32 devices in a mesh: dp: 4 (over y, x), tr: 2 (over core), tc: 4 (over z).
Axes of the slice: x: 2, y: 2, z: 4, core: 2. Of those that a mesh axis runs over, the one named last changes fastest.
Arguments:
- activations: bfloat16 [4096, 3072], P(('dp', 'tc'), 'tr'), may hold values from -6 to 6
- cotangent: bfloat16 [4096, 8192], P(('dp', 'tr'), 'tc'), may hold values from -0.09375 to 0.09375
- master: float32 [2, 1536, 8192], P('tr', ('dp', 'tc')), may hold values from -3 to 3
- moment: float32 [2, 1536, 8192], P('tr', ('dp', 'tc')), may hold values from -2 to 2
- second: float32 [2, 1536, 8192], P('tr', ('dp', 'tc')), may hold values from 0.05 to 2
Outputs:
- new_master: float32 [2, 1536, 8192], P('tr', ('dp', 'tc'))
- new_moment: float32 [2, 1536, 8192], P('tr', ('dp', 'tc'))
- new_second: float32 [2, 1536, 8192], P('tr', ('dp', 'tc'))
The draws below stay inside these ranges and needn't reach their ends.
All inputs are finite; a program needn't handle non-finite values.
Results may differ from the reference program's by a relative error of at most 0.0003.
Values may be sent and summed in bfloat16 or wider, within the bound.
A program may use at most 128 MiB of HBM per device.

```python
import math
import jax
import jax.numpy as jnp
from jax import lax

D = 3072
FFW = 8192
TOK_REP = 1024
TOKENS = 4096
N_DP = 4
N_TR = 2


def strengthened(array, stream_key, source, target, parts, factor):
    def block_of(position):
        return (jnp.arange(array.shape[position]) // (array.shape[position] // parts)).reshape((-1,) + (1,) * (array.ndim - 1 - position))

    one_side = jax.random.permutation(stream_key, parts)[block_of(target)]
    second = (block_of(target) + parts // 2) % parts
    return jnp.where((block_of(source) == one_side) | (block_of(source) == second), factor * array, array)


def level_of(key, dims, shards, least, largest):
    def one(position, blocks):
        heights = jax.random.uniform(jax.random.fold_in(jax.random.fold_in(key, 6), position), (blocks,), jnp.float32, least / len(shards), largest / len(shards))
        return jnp.repeat(jnp.exp(heights), dims[position] // blocks).reshape((-1,) + (1,) * (len(dims) - position - 1))

    level = one(*shards[0])
    for cut in shards[1:]:
        level = level * one(*cut)
    return level


def centred(rng, shape, width, reach, shards=(), dtype=jnp.bfloat16):
    array = width * jax.random.normal(rng, shape, jnp.float32)
    if shards:
        array = array * level_of(rng, shape, shards, -0.22, 0.18)
    return jnp.clip(array, -reach, reach).astype(dtype)


def heavy_noise(stream_key, shape, width, limit, cuts, heavy, held_as=jnp.bfloat16):
    drawn = width * jax.random.normal(stream_key, shape, jnp.float32)
    if cuts:
        drawn = drawn * level_of(stream_key, shape, cuts, -0.22, 0.18)
    return jnp.clip(strengthened(drawn, jax.random.fold_in(stream_key, 3), *heavy), -limit, limit).astype(held_as)


def setup_inputs(seed: int = 0) -> dict:
    key_of = jax.random.split(jax.random.key(seed), 6)
    return {
        "activations": heavy_noise(key_of[0], (TOKENS, D), 1.0, 6.0, ((0, 16), (1, 2)), (0, 1, 16, 2.0)),
        "cotangent": centred(key_of[1], (TOKENS, FFW), TOKENS ** -0.5, 0.09375, ((0, 8), (1, 4))),
        "master": centred(key_of[2], (N_TR, D // N_TR, FFW), 0.5, 3.0, ((0, 2), (1, 16)), jnp.float32),
        "moment": centred(key_of[3], (N_TR, D // N_TR, FFW), 0.3, 2.0, ((0, 2), (1, 16)), jnp.float32),
        "second": jnp.clip(jnp.exp(math.log(2.0) - 3.6888794 * jax.random.uniform(key_of[4], (N_TR, D // N_TR, FFW), jnp.float32) ** level_of(key_of[4], (N_TR, D // N_TR, FFW), ((0, 2), (1, 16)), -0.2, 0.2)), 0.05, 2.0),
    }


first_decay = 0.9
second_decay = 0.95
learn_rate = 0.0003
weight_decay = 0.1
epsilon = 1e-08
first_fix = 1.0 - 0.9 ** 10
second_fix = 1.0 - 0.95 ** 10

def reference(activations, cotangent, master, moment, second):
    blocks_x = activations.reshape(N_DP, TOK_REP, D)
    blocks_y = cotangent.reshape(N_DP, TOK_REP, FFW)

    def accumulate(total, pair):
        return (total + jnp.dot(pair[0].T, pair[1], preferred_element_type=jnp.float32), None)
    grad, unused = lax.scan(accumulate, jnp.zeros((D, FFW), jnp.float32), (blocks_x, blocks_y))
    grad = grad.reshape(N_TR, D // N_TR, FFW)
    new_moment = first_decay * moment + (1.0 - first_decay) * grad
    new_second = second_decay * second + (1.0 - second_decay) * grad * grad
    update = new_moment / first_fix / (jnp.sqrt(new_second / second_fix) + epsilon)
    new_master = master - learn_rate * (update + weight_decay * master)
    return (new_master, new_moment, new_second)
```

```python
import functools

import jax
import jax.numpy as jnp
from jax import lax
from jax.experimental import pallas as pl
from jax.experimental.pallas import tpu as pltpu
from jax.sharding import PartitionSpec as P

first_decay = 0.9
second_decay = 0.95
learn_rate = 0.0003
weight_decay = 0.1
epsilon = 1e-08
first_fix = 1.0 - 0.9**10
second_fix = 1.0 - 0.95**10

MESH = pl.DeviceIdType.MESH
VMEM_BYTES = 60 * 2**20
CHUNKS = 4
SCALE = 1.0
WIRE = jnp.float32


def grad_kernel(sizes, act, cot, out, abuf, cbuf, at, obuf, ld_sem, adp_s, adp_r, az_s, az_r, c_s, c_r, o_s, o_r):
    dp, tr, tc, chunks, tile = sizes
    r, c, z = lax.axis_index("dp"), lax.axis_index("tr"), lax.axis_index("tc")
    rx = r + 1 - 2 * lax.rem(r, 2)
    ry = lax.rem(r + 2, 4)
    rd = 3 - r
    rel = (r, rx, ry, rd)
    atok, rows = abuf.shape[2], abuf.shape[3]
    ctok, nu = cbuf.shape[3], cbuf.shape[4]
    units = chunks * nu
    half = ctok // 2

    barrier = pltpu.get_barrier_semaphore()
    peers = [{"dp": q} for q in (rx, ry, rd)] + [{"tr": 1 - c}]
    peers += [{"tc": lax.rem(z + j, tc)} for j in range(1, tc)]
    for peer in peers:
        pl.semaphore_signal(barrier, inc=1, device_id=peer, device_id_type=MESH)
    pl.semaphore_wait(barrier, len(peers))

    def remote(src, dst, s, d, peer):
        return pltpu.make_async_remote_copy(
            src_ref=src, dst_ref=dst, send_sem=s, recv_sem=d, device_id=peer, device_id_type=MESH
        )

    def act_cols(q):
        return act.at[:, pl.ds(pl.multiple_of(q * rows, 128), rows)]

    def a_dp(k):
        return remote(act_cols(rel[k]), abuf.at[r, z], adp_s.at[k], adp_r.at[k], {"dp": rel[k]})

    def a_z(d, s, k):
        block = z - s if d == 0 else z + s
        to = z + 1 if d == 0 else z - 1
        slot = abuf.at[rel[k], block]
        src = act_cols(r) if s == 0 and k == 0 else slot
        return remote(src, slot, az_s.at[d, s, k], az_r.at[d, s, k], {"tc": to})

    def a_z_sends(d, s):
        return (z >= s) & (z < tc - 1) if d == 0 else (z < tc - s) & (z > 0)

    def a_z_gets(d, s):
        return z >= s + 1 if d == 0 else z < tc - 1 - s

    def send_z(s, k):
        for d in range(2):
            @pl.when(a_z_sends(d, s))
            def _():
                a_z(d, s, k).start()

    def got_z(s, k):
        for d in range(2):
            @pl.when(a_z_gets(d, s))
            def _():
                a_z(d, s, k).wait_recv()

    def cot_cols(u):
        return cot.at[:, pl.ds(u * nu, nu)]

    def c_copy(flow, u):
        if flow == 0:
            return remote(cot_cols(u), cbuf.at[u, r, c], c_s.at[0, u], c_r.at[0, u], {"dp": rx})
        if flow == 1:
            return remote(cot_cols(u), cbuf.at[u, r, c], c_s.at[1, u], c_r.at[1, u], {"dp": ry})
        if flow == 2:
            part = cbuf.at[u, ry, c, pl.ds(0, half)]
            return remote(part, part, c_s.at[2, u], c_r.at[2, u], {"dp": rx})
        if flow == 3:
            part = cbuf.at[u, rx, c, pl.ds(half, half)]
            return remote(part, part, c_s.at[3, u], c_r.at[3, u], {"dp": ry})
        k = flow - 4
        slot = cbuf.at[u, rel[k], c]
        src = cot_cols(u) if k == 0 else slot
        return remote(src, slot, c_s.at[flow, u], c_r.at[flow, u], {"tr": 1 - c})

    def own(u):
        for flow in (0, 1, 4):
            c_copy(flow, u).start()

    def got_xy(u):
        c_copy(0, u).wait_recv()
        c_copy(3, u).start()
        c_copy(5, u).start()
        c_copy(1, u).wait_recv()
        c_copy(2, u).start()
        c_copy(6, u).start()

    def got_diag(u):
        c_copy(2, u).wait_recv()
        c_copy(3, u).wait_recv()
        c_copy(7, u).start()

    def local_c(u):
        return pltpu.make_async_copy(cot_cols(u), cbuf.at[u, r, c], ld_sem.at[1 + u])

    local_a = pltpu.make_async_copy(act_cols(r), abuf.at[r, z], ld_sem.at[0])

    def o_copy(j, u):
        to = lax.rem(z + j, tc)
        dst = out.at[:, pl.ds(pl.multiple_of(z * units + u * nu, 128), nu)]
        if j == 0:
            return pltpu.make_async_copy(obuf.at[u, z], dst, o_s.at[0, u])
        return remote(obuf.at[u, to], dst, o_s.at[j, u], o_r.at[j, u], {"tc": to})

    owned = rows // tc

    def compute(u):
        for flow in range(4, 8):
            c_copy(flow, u).wait_recv()
        local_c(u).wait()

        @pl.loop(0, nu // tile)
        def _(t):
            cols = pl.ds(pl.multiple_of(t * tile, tile), tile)
            total = jnp.zeros((rows, tile), jnp.float32)
            for q in range(dp):
                rhs = cbuf[u, q, :, :, cols].reshape(tr * ctok, tile)
                total += jnp.dot(at[q], rhs, preferred_element_type=jnp.float32)
            total = (total * SCALE).astype(WIRE)
            for j in range(tc):
                obuf[u, j, :, cols] = total[j * owned:(j + 1) * owned]

        for j in (*range(1, tc), 0):
            o_copy(j, u).start()

    for k in range(1, 4):
        a_dp(k).start()
    send_z(0, 0)
    own(0)
    own(1)
    local_a.start()
    for u in range(chunks):
        local_c(u).start()
    for k in range(1, 4):
        a_dp(k).wait_recv()
        send_z(0, k)

    def forward(s, k):
        got_z(s - 1, k)
        send_z(s, k)

    def step_xy(u):
        got_xy(u)
        if u + 2 < chunks:
            own(u + 2)

    def last_a(k):
        got_z(tc - 2, k)
        if k == 0:
            local_a.wait()
        at[rel[k]] = abuf[rel[k]].reshape(tc * atok, rows).T

    moves = [(forward, s, k) for s in range(1, tc - 1) for k in range(4)]
    moves += [(last_a, k) for k in range(4)]
    turns = []
    for u in range(chunks):
        turns.append((step_xy, u))
        if u >= 1:
            turns.append((got_diag, u - 1))
    order = []
    early = 2 * (chunks // 2)
    for i, move in enumerate(moves):
        order.append(move)
        if i >= 2 and turns and (i - 2) % (len(moves) // early) == 0 and len(turns) > chunks // 2:
            order.append(turns.pop(0))
    for f, *args in order:
        f(*args)
    done = 0
    for f, u in turns:
        f(u)
        if f is got_diag:
            while done <= u:
                compute(done)
                done += 1
    got_diag(chunks - 1)
    while done < chunks:
        compute(done)
        done += 1

    for k in range(1, 4):
        a_dp(k).wait_send()
    for d in range(2):
        for s in range(tc - 1):
            @pl.when(a_z_sends(d, s))
            def _():
                for k in range(4):
                    a_z(d, s, k).wait_send()
    for u in range(chunks):
        for flow in range(8):
            c_copy(flow, u).wait_send()
    for u in range(chunks):
        o_copy(0, u).wait()
        for j in range(1, tc):
            o_copy(j, u).wait_send()
            o_copy(j, u).wait_recv()


def vmem_plan(activations, cotangent, dp, tr, tc):
    atok, features = activations.shape
    ctok, units = cotangent.shape
    rows = features // dp
    return dp * tc * atok * rows * 4 + dp * tr * ctok * units * 2 + rows * units * 2


def gathered(activations, cotangent, dp, tr, tc):
    atok, features = activations.shape
    ctok, units = cotangent.shape
    rows = features // dp
    owned = rows // tc
    chunks = CHUNKS
    nu = units // chunks
    tile = min(nu, 256)
    return pl.pallas_call(
        functools.partial(grad_kernel, (dp, tr, tc, chunks, tile)),
        out_shape=jax.ShapeDtypeStruct((owned, tc * units), WIRE),
        in_specs=[pl.BlockSpec(memory_space=pl.ANY)] * 2,
        out_specs=pl.BlockSpec(memory_space=pl.ANY),
        scratch_shapes=[
            pltpu.VMEM((dp, tc, atok, rows), jnp.bfloat16),
            pltpu.VMEM((chunks, dp, tr, ctok, nu), jnp.bfloat16),
            pltpu.VMEM((dp, rows, tc * atok), jnp.bfloat16),
            pltpu.VMEM((chunks, tc, owned, nu), WIRE),
            pltpu.SemaphoreType.DMA((1 + chunks,)),
            pltpu.SemaphoreType.DMA((4,)),
            pltpu.SemaphoreType.DMA((4,)),
            pltpu.SemaphoreType.DMA((2, tc - 1, 4)),
            pltpu.SemaphoreType.DMA((2, tc - 1, 4)),
            pltpu.SemaphoreType.DMA((8, chunks)),
            pltpu.SemaphoreType.DMA((8, chunks)),
            pltpu.SemaphoreType.DMA((tc, chunks)),
            pltpu.SemaphoreType.DMA((tc, chunks)),
        ],
        compiler_params=pltpu.CompilerParams(
            collective_id=0, has_side_effects=True, vmem_limit_bytes=VMEM_BYTES
        ),
    )(activations, cotangent)


def native(activations, cotangent):
    act_rows = lax.all_gather(activations, "tc", axis=0, tiled=True)
    cot_rows = lax.all_gather(cotangent, "tr", axis=0, tiled=True)
    replicas = lax.axis_size("dp")
    columns = lax.axis_size("tc")
    feature_count = act_rows.shape[1]
    unit_count = cot_rows.shape[1]
    owned = feature_count // (replicas * columns)
    summed = lax.psum_scatter(
        lax.dot_general(
            act_rows, cot_rows, (((0,), (0,)), ((), ())), preferred_element_type=jnp.float32
        ),
        "dp",
        scatter_dimension=0,
        tiled=True,
    )
    summed = summed.reshape(columns, owned, unit_count)
    return lax.all_to_all(summed, "tc", split_axis=0, concat_axis=2, tiled=True)


def shards(activations, cotangent, master, moment, second):
    dp, tr, tc = (lax.axis_size(name) for name in ("dp", "tr", "tc"))
    small = vmem_plan(activations, cotangent, dp, tr, tc) < VMEM_BYTES * 3 // 4
    if dp == 4 and tr == 2 and tc > 2 and small:
        grad = gathered(activations, cotangent, dp, tr, tc)
        grad = (grad.astype(jnp.float32) * (1.0 / SCALE)).reshape(master.shape)
    else:
        grad = native(activations, cotangent)
    new_moment = first_decay * moment + (1.0 - first_decay) * grad
    new_second = second_decay * second + (1.0 - second_decay) * grad * grad
    update = new_moment / first_fix / (jnp.sqrt(new_second / second_fix) + epsilon)
    new_master = master - learn_rate * (update + weight_decay * master)
    return (new_master, new_moment, new_second)


def solution(mesh):
    return jax.shard_map(
        shards,
        mesh=mesh,
        in_specs=(
            P(("dp", "tc"), "tr"),
            P(("dp", "tr"), "tc"),
            P("tr", ("dp", "tc"), None),
            P("tr", ("dp", "tc"), None),
            P("tr", ("dp", "tc"), None),
        ),
        out_specs=(
            P("tr", ("dp", "tc"), None),
            P("tr", ("dp", "tc"), None),
            P("tr", ("dp", "tc"), None),
        ),
        check_vma=False,
    )
```

```python
import functools

import jax
import jax.numpy as jnp
from jax import lax
from jax.experimental import pallas as pl
from jax.experimental.pallas import tpu as pltpu
from jax.sharding import PartitionSpec as P

first_decay = 0.9
second_decay = 0.95
learn_rate = 0.0003
weight_decay = 0.1
epsilon = 1e-08
first_fix = 1.0 - 0.9**10
second_fix = 1.0 - 0.95**10

MESH = pl.DeviceIdType.MESH
VMEM_BYTES = 60 * 2**20
CHUNKS = 4
LEVELS = 12.0
STEPS = 128.0 * LEVELS


def encode(v):
    y = jnp.abs(v) * 2.0**8
    tiny = y < 1.0
    y = jnp.where(tiny, y + 1.0, y)
    high = y >= 2.0**16
    power = jnp.where(high, 2.0**78, jnp.where(tiny, 2.0**-126, 2.0**-114))
    y = jnp.where(high, y * 2.0**-16, y)
    for s in (8, 4, 2, 1):
        big = y >= 2.0**s
        y = jnp.where(big, y * 2.0**-s, y)
        power = jnp.where(big, power * 2.0 ** (12 * s), power)
    step = jnp.minimum(jnp.floor((y - 1.0) * STEPS + 0.5), STEPS - 1.0)
    quotient = jnp.floor((step + 0.5) * (1.0 / LEVELS))
    rest = step - LEVELS * quotient
    for s in (8, 4, 2, 1):
        big = rest >= s
        rest = jnp.where(big, rest - s, rest)
        power = jnp.where(big, power * 2.0**s, power)
    code = power * (1.0 + quotient * (1.0 / 128.0))
    return jnp.where(v < 0.0, -code, code).astype(jnp.bfloat16)


def decode(code):
    code = code.astype(jnp.float32)
    x = jnp.abs(code)
    top, mid = x >= 2.0**66, x >= 2.0**-30
    x = x * jnp.where(top, 2.0**-66, jnp.where(mid, 2.0**30, 2.0**126))
    power = jnp.where(top, 2.0**15, jnp.where(mid, 2.0**7, 2.0**-1))
    for s in (4, 2, 1):
        big = x >= 2.0 ** (12 * s)
        x = jnp.where(big, x * 2.0 ** (-12 * s), x)
        power = jnp.where(big, power * 2.0**s, power)
    rest = jnp.zeros_like(x)
    for s in (8, 4, 2, 1):
        big = x >= 2.0**s
        x = jnp.where(big, x * 2.0**-s, x)
        rest = jnp.where(big, rest + s, rest)
    x = x + rest * (1.0 / STEPS)
    y = jnp.where(power < 1.0, x - 1.0, x * power) * 2.0**-8
    return jnp.where(code < 0.0, -y, y)


def grad_kernel(sizes, act, cot, out, abuf, cbuf, at, obuf, rbuf, dbuf, ld_sem, adp_s, adp_r, az_s, az_r, c_s, c_r, o_s, o_r, st_sem):
    dp, tr, tc, chunks, tile = sizes
    r, c, z = lax.axis_index("dp"), lax.axis_index("tr"), lax.axis_index("tc")
    rx = r + 1 - 2 * lax.rem(r, 2)
    ry = lax.rem(r + 2, 4)
    rd = 3 - r
    rel = (r, rx, ry, rd)
    atok, rows = abuf.shape[2], abuf.shape[3]
    ctok, nu = cbuf.shape[3], cbuf.shape[4]
    units = chunks * nu
    half = ctok // 2

    barrier = pltpu.get_barrier_semaphore()
    peers = [{"dp": q} for q in (rx, ry, rd)] + [{"tr": 1 - c}]
    peers += [{"tc": lax.rem(z + j, tc)} for j in range(1, tc)]
    for peer in peers:
        pl.semaphore_signal(barrier, inc=1, device_id=peer, device_id_type=MESH)
    pl.semaphore_wait(barrier, len(peers))

    def remote(src, dst, s, d, peer):
        return pltpu.make_async_remote_copy(
            src_ref=src, dst_ref=dst, send_sem=s, recv_sem=d, device_id=peer, device_id_type=MESH
        )

    def act_cols(q):
        return act.at[:, pl.ds(pl.multiple_of(q * rows, 128), rows)]

    def a_dp(k):
        return remote(act_cols(rel[k]), abuf.at[r, z], adp_s.at[k], adp_r.at[k], {"dp": rel[k]})

    def a_z(d, s, k):
        block = z - s if d == 0 else z + s
        to = z + 1 if d == 0 else z - 1
        slot = abuf.at[rel[k], block]
        src = act_cols(r) if s == 0 and k == 0 else slot
        return remote(src, slot, az_s.at[d, s, k], az_r.at[d, s, k], {"tc": to})

    def a_z_sends(d, s):
        return (z >= s) & (z < tc - 1) if d == 0 else (z < tc - s) & (z > 0)

    def a_z_gets(d, s):
        return z >= s + 1 if d == 0 else z < tc - 1 - s

    def send_z(s, k):
        for d in range(2):
            @pl.when(a_z_sends(d, s))
            def _():
                a_z(d, s, k).start()

    def got_z(s, k):
        for d in range(2):
            @pl.when(a_z_gets(d, s))
            def _():
                a_z(d, s, k).wait_recv()

    def cot_cols(u):
        return cot.at[:, pl.ds(u * nu, nu)]

    def c_copy(flow, u):
        if flow == 0:
            return remote(cot_cols(u), cbuf.at[u, r, c], c_s.at[0, u], c_r.at[0, u], {"dp": rx})
        if flow == 1:
            return remote(cot_cols(u), cbuf.at[u, r, c], c_s.at[1, u], c_r.at[1, u], {"dp": ry})
        if flow == 2:
            part = cbuf.at[u, ry, c, pl.ds(0, half)]
            return remote(part, part, c_s.at[2, u], c_r.at[2, u], {"dp": rx})
        if flow == 3:
            part = cbuf.at[u, rx, c, pl.ds(half, half)]
            return remote(part, part, c_s.at[3, u], c_r.at[3, u], {"dp": ry})
        k = flow - 4
        slot = cbuf.at[u, rel[k], c]
        src = cot_cols(u) if k == 0 else slot
        return remote(src, slot, c_s.at[flow, u], c_r.at[flow, u], {"tr": 1 - c})

    def own(u):
        for flow in (0, 1, 4):
            c_copy(flow, u).start()

    def got_xy(u):
        c_copy(0, u).wait_recv()
        c_copy(3, u).start()
        c_copy(5, u).start()
        c_copy(1, u).wait_recv()
        c_copy(2, u).start()
        c_copy(6, u).start()

    def got_diag(u):
        c_copy(2, u).wait_recv()
        c_copy(3, u).wait_recv()
        c_copy(7, u).start()

    def local_c(u):
        return pltpu.make_async_copy(cot_cols(u), cbuf.at[u, r, c], ld_sem.at[1 + u])

    local_a = pltpu.make_async_copy(act_cols(r), abuf.at[r, z], ld_sem.at[0])

    def o_copy(j, u):
        to = lax.rem(z + j, tc)
        return remote(obuf.at[u, to], rbuf.at[u, z], o_s.at[j, u], o_r.at[j, u], {"tc": to})

    def store(block, j, u):
        dst = out.at[:, pl.ds(pl.multiple_of(block * units + u * nu, 128), nu)]
        return pltpu.make_async_copy(dbuf.at[u, block], dst, st_sem.at[j, u])

    owned = rows // tc

    def compute(u):
        for flow in range(4, 8):
            c_copy(flow, u).wait_recv()
        local_c(u).wait()

        @pl.loop(0, nu // tile)
        def _(t):
            cols = pl.ds(pl.multiple_of(t * tile, tile), tile)
            total = jnp.zeros((rows, tile), jnp.float32)
            for q in range(dp):
                rhs = cbuf[u, q, :, :, cols].reshape(tr * ctok, tile)
                total += jnp.dot(at[q], rhs, preferred_element_type=jnp.float32)
            for j in range(tc):
                part = total[j * owned:(j + 1) * owned]
                obuf[u, j, :, cols] = encode(part)

                @pl.when(z == j)
                def _():
                    dbuf[u, j, :, cols] = part

        for j in range(1, tc):
            o_copy(j, u).start()
        store(z, 0, u).start()

    def finish(u):
        for j in range(1, tc):
            o_copy(j, u).wait_recv()
            block = lax.rem(z + tc - j, tc)

            @pl.loop(0, owned // 16)
            def _(i):
                part = pl.ds(pl.multiple_of(i * 16, 16), 16)
                dbuf[u, block, part] = decode(rbuf[u, block, part])

            store(block, j, u).start()

    for k in range(1, 4):
        a_dp(k).start()
    send_z(0, 0)
    own(0)
    own(1)
    local_a.start()
    for u in range(chunks):
        local_c(u).start()
    for k in range(1, 4):
        a_dp(k).wait_recv()
        send_z(0, k)

    def forward(s, k):
        got_z(s - 1, k)
        send_z(s, k)

    def step_xy(u):
        got_xy(u)
        if u + 2 < chunks:
            own(u + 2)

    def last_a(k):
        got_z(tc - 2, k)
        if k == 0:
            local_a.wait()
        at[rel[k]] = abuf[rel[k]].reshape(tc * atok, rows).T

    moves = [(forward, s, k) for s in range(1, tc - 1) for k in range(4)]
    moves += [(last_a, k) for k in range(4)]
    turns = []
    for u in range(chunks):
        turns.append((step_xy, u))
        if u >= 1:
            turns.append((got_diag, u - 1))
    order = []
    early = 2 * (chunks // 2)
    for i, move in enumerate(moves):
        order.append(move)
        if i >= 2 and turns and (i - 2) % (len(moves) // early) == 0 and len(turns) > chunks // 2:
            order.append(turns.pop(0))
    for f, *args in order:
        f(*args)
    done = 0
    for f, u in turns:
        f(u)
        if f is got_diag:
            while done <= u:
                compute(done)
                done += 1
    got_diag(chunks - 1)
    while done < chunks:
        compute(done)
        done += 1
    for u in range(chunks):
        finish(u)

    for k in range(1, 4):
        a_dp(k).wait_send()
    for d in range(2):
        for s in range(tc - 1):
            @pl.when(a_z_sends(d, s))
            def _():
                for k in range(4):
                    a_z(d, s, k).wait_send()
    for u in range(chunks):
        for flow in range(8):
            c_copy(flow, u).wait_send()
    for u in range(chunks):
        store(z, 0, u).wait()
        for j in range(1, tc):
            o_copy(j, u).wait_send()
            store(lax.rem(z + tc - j, tc), j, u).wait()


def vmem_plan(activations, cotangent, dp, tr, tc):
    atok, features = activations.shape
    ctok, units = cotangent.shape
    rows = features // dp
    return dp * tc * atok * rows * 4 + dp * tr * ctok * units * 2 + rows * units * 8


def gathered(activations, cotangent, dp, tr, tc):
    atok, features = activations.shape
    ctok, units = cotangent.shape
    rows = features // dp
    owned = rows // tc
    chunks = CHUNKS
    nu = units // chunks
    tile = min(nu, 256)
    return pl.pallas_call(
        functools.partial(grad_kernel, (dp, tr, tc, chunks, tile)),
        out_shape=jax.ShapeDtypeStruct((owned, tc * units), jnp.float32),
        in_specs=[pl.BlockSpec(memory_space=pl.ANY)] * 2,
        out_specs=pl.BlockSpec(memory_space=pl.ANY),
        scratch_shapes=[
            pltpu.VMEM((dp, tc, atok, rows), jnp.bfloat16),
            pltpu.VMEM((chunks, dp, tr, ctok, nu), jnp.bfloat16),
            pltpu.VMEM((dp, rows, tc * atok), jnp.bfloat16),
            pltpu.VMEM((chunks, tc, owned, nu), jnp.bfloat16),
            pltpu.VMEM((chunks, tc, owned, nu), jnp.bfloat16),
            pltpu.VMEM((chunks, tc, owned, nu), jnp.float32),
            pltpu.SemaphoreType.DMA((1 + chunks,)),
            pltpu.SemaphoreType.DMA((4,)),
            pltpu.SemaphoreType.DMA((4,)),
            pltpu.SemaphoreType.DMA((2, tc - 1, 4)),
            pltpu.SemaphoreType.DMA((2, tc - 1, 4)),
            pltpu.SemaphoreType.DMA((8, chunks)),
            pltpu.SemaphoreType.DMA((8, chunks)),
            pltpu.SemaphoreType.DMA((tc, chunks)),
            pltpu.SemaphoreType.DMA((tc, chunks)),
            pltpu.SemaphoreType.DMA((tc, chunks)),
        ],
        compiler_params=pltpu.CompilerParams(
            collective_id=0, has_side_effects=True, vmem_limit_bytes=VMEM_BYTES
        ),
    )(activations, cotangent)


def native(activations, cotangent):
    act_rows = lax.all_gather(activations, "tc", axis=0, tiled=True)
    cot_rows = lax.all_gather(cotangent, "tr", axis=0, tiled=True)
    replicas = lax.axis_size("dp")
    columns = lax.axis_size("tc")
    feature_count = act_rows.shape[1]
    unit_count = cot_rows.shape[1]
    owned = feature_count // (replicas * columns)
    summed = lax.psum_scatter(
        lax.dot_general(
            act_rows, cot_rows, (((0,), (0,)), ((), ())), preferred_element_type=jnp.float32
        ),
        "dp",
        scatter_dimension=0,
        tiled=True,
    )
    summed = summed.reshape(columns, owned, unit_count)
    return lax.all_to_all(summed, "tc", split_axis=0, concat_axis=2, tiled=True)


def shards(activations, cotangent, master, moment, second):
    dp, tr, tc = (lax.axis_size(name) for name in ("dp", "tr", "tc"))
    small = vmem_plan(activations, cotangent, dp, tr, tc) < VMEM_BYTES * 3 // 4
    if dp == 4 and tr == 2 and tc > 2 and small:
        grad = gathered(activations, cotangent, dp, tr, tc)
        grad = grad.reshape(master.shape)
    else:
        grad = native(activations, cotangent)
    new_moment = first_decay * moment + (1.0 - first_decay) * grad
    new_second = second_decay * second + (1.0 - second_decay) * grad * grad
    update = new_moment / first_fix / (jnp.sqrt(new_second / second_fix) + epsilon)
    new_master = master - learn_rate * (update + weight_decay * master)
    return (new_master, new_moment, new_second)


def solution(mesh):
    return jax.shard_map(
        shards,
        mesh=mesh,
        in_specs=(
            P(("dp", "tc"), "tr"),
            P(("dp", "tr"), "tc"),
            P("tr", ("dp", "tc"), None),
            P("tr", ("dp", "tc"), None),
            P("tr", ("dp", "tc"), None),
        ),
        out_specs=(
            P("tr", ("dp", "tc"), None),
            P("tr", ("dp", "tc"), None),
            P("tr", ("dp", "tc"), None),
        ),
        check_vma=False,
    )
```

```python
import functools

import jax
import jax.numpy as jnp
from jax import lax
from jax.experimental import pallas as pl
from jax.experimental.pallas import tpu as pltpu
from jax.sharding import PartitionSpec as P

first_decay = 0.9
second_decay = 0.95
learn_rate = 0.0003
weight_decay = 0.1
epsilon = 1e-08
first_fix = 1.0 - 0.9**10
second_fix = 1.0 - 0.95**10

MESH = pl.DeviceIdType.MESH
VMEM_BYTES = 40 * 2**20
CHUNKS = 8
AHEAD = 2
LEVELS = 12.0
STEPS = 128.0 * LEVELS


def encode(v):
    y = jnp.abs(v) * 2.0**8
    tiny = y < 1.0
    y = jnp.where(tiny, y + 1.0, y)
    high = y >= 2.0**16
    power = jnp.where(high, 2.0**78, jnp.where(tiny, 2.0**-126, 2.0**-114))
    y = jnp.where(high, y * 2.0**-16, y)
    for s in (8, 4, 2, 1):
        big = y >= 2.0**s
        y = jnp.where(big, y * 2.0**-s, y)
        power = jnp.where(big, power * 2.0 ** (12 * s), power)
    step = jnp.minimum(jnp.floor((y - 1.0) * STEPS + 0.5), STEPS - 1.0)
    quotient = jnp.floor((step + 0.5) * (1.0 / LEVELS))
    rest = step - LEVELS * quotient
    for s in (8, 4, 2, 1):
        big = rest >= s
        rest = jnp.where(big, rest - s, rest)
        power = jnp.where(big, power * 2.0**s, power)
    code = power * (1.0 + quotient * (1.0 / 128.0))
    return jnp.where(v < 0.0, -code, code).astype(jnp.bfloat16)


def decode(code):
    code = code.astype(jnp.float32)
    x = jnp.abs(code)
    top, mid = x >= 2.0**66, x >= 2.0**-30
    x = x * jnp.where(top, 2.0**-66, jnp.where(mid, 2.0**30, 2.0**126))
    power = jnp.where(top, 2.0**15, jnp.where(mid, 2.0**7, 2.0**-1))
    for s in (4, 2, 1):
        big = x >= 2.0 ** (12 * s)
        x = jnp.where(big, x * 2.0 ** (-12 * s), x)
        power = jnp.where(big, power * 2.0**s, power)
    rest = jnp.zeros_like(x)
    for s in (8, 4, 2, 1):
        big = x >= 2.0**s
        x = jnp.where(big, x * 2.0**-s, x)
        rest = jnp.where(big, rest + s, rest)
    x = x + rest * (1.0 / STEPS)
    y = jnp.where(power < 1.0, x - 1.0, x * power) * 2.0**-8
    return jnp.where(code < 0.0, -y, y)


def grad_kernel(sizes, act, cot, out, abuf, cbuf, at, obuf, rbuf, dbuf, ld_sem, adp_s, adp_r, az_s, az_r, c_s, c_r, o_s, o_r, st_sem):
    dp, tr, tc, chunks, tile = sizes
    r, c, z = lax.axis_index("dp"), lax.axis_index("tr"), lax.axis_index("tc")
    rx = r + 1 - 2 * lax.rem(r, 2)
    ry = lax.rem(r + 2, 4)
    rd = 3 - r
    rel = (r, rx, ry, rd)
    atok, rows = abuf.shape[2], abuf.shape[3]
    ctok, nu = cbuf.shape[3], cbuf.shape[4]
    units = chunks * nu
    half = ctok // 2

    barrier = pltpu.get_barrier_semaphore()
    peers = [{"dp": q} for q in (rx, ry, rd)] + [{"tr": 1 - c}]
    peers += [{"tc": lax.rem(z + j, tc)} for j in range(1, tc)]
    for peer in peers:
        pl.semaphore_signal(barrier, inc=1, device_id=peer, device_id_type=MESH)
    pl.semaphore_wait(barrier, len(peers))

    def remote(src, dst, s, d, peer):
        return pltpu.make_async_remote_copy(
            src_ref=src, dst_ref=dst, send_sem=s, recv_sem=d, device_id=peer, device_id_type=MESH
        )

    def act_cols(q):
        return act.at[:, pl.ds(pl.multiple_of(q * rows, 128), rows)]

    def a_dp(k):
        return remote(act_cols(rel[k]), abuf.at[r, z], adp_s.at[k], adp_r.at[k], {"dp": rel[k]})

    def a_z(d, s, k):
        block = z - s if d == 0 else z + s
        to = z + 1 if d == 0 else z - 1
        slot = abuf.at[rel[k], block]
        src = act_cols(r) if s == 0 and k == 0 else slot
        return remote(src, slot, az_s.at[d, s, k], az_r.at[d, s, k], {"tc": to})

    def a_z_sends(d, s):
        return (z >= s) & (z < tc - 1) if d == 0 else (z < tc - s) & (z > 0)

    def a_z_gets(d, s):
        return z >= s + 1 if d == 0 else z < tc - 1 - s

    def send_z(s, k):
        for d in range(2):
            @pl.when(a_z_sends(d, s))
            def _():
                a_z(d, s, k).start()

    def got_z(s, k):
        for d in range(2):
            @pl.when(a_z_gets(d, s))
            def _():
                a_z(d, s, k).wait_recv()

    def cot_cols(u):
        return cot.at[:, pl.ds(u * nu, nu)]

    def c_copy(flow, u):
        if flow == 0:
            return remote(cot_cols(u), cbuf.at[u, r, c], c_s.at[0, u], c_r.at[0, u], {"dp": rx})
        if flow == 1:
            return remote(cot_cols(u), cbuf.at[u, r, c], c_s.at[1, u], c_r.at[1, u], {"dp": ry})
        if flow == 2:
            part = cbuf.at[u, ry, c, pl.ds(0, half)]
            return remote(part, part, c_s.at[2, u], c_r.at[2, u], {"dp": rx})
        if flow == 3:
            part = cbuf.at[u, rx, c, pl.ds(half, half)]
            return remote(part, part, c_s.at[3, u], c_r.at[3, u], {"dp": ry})
        k = flow - 4
        slot = cbuf.at[u, rel[k], c]
        src = cot_cols(u) if k == 0 else slot
        return remote(src, slot, c_s.at[flow, u], c_r.at[flow, u], {"tr": 1 - c})

    def own(u):
        for flow in (0, 1, 4):
            c_copy(flow, u).start()

    def got_xy(u):
        c_copy(0, u).wait_recv()
        c_copy(3, u).start()
        c_copy(5, u).start()
        c_copy(1, u).wait_recv()
        c_copy(2, u).start()
        c_copy(6, u).start()

    def got_diag(u):
        c_copy(2, u).wait_recv()
        c_copy(3, u).wait_recv()
        c_copy(7, u).start()

    def local_c(u):
        return pltpu.make_async_copy(cot_cols(u), cbuf.at[u, r, c], ld_sem.at[1 + u])

    local_a = pltpu.make_async_copy(act_cols(r), abuf.at[r, z], ld_sem.at[0])

    def o_copy(j, u):
        to = lax.rem(z + j, tc)
        return remote(obuf.at[u, to], rbuf.at[u, z], o_s.at[j, u], o_r.at[j, u], {"tc": to})

    def store(block, j, u):
        dst = out.at[:, pl.ds(pl.multiple_of(block * units + u * nu, 128), nu)]
        return pltpu.make_async_copy(dbuf.at[u, block], dst, st_sem.at[j, u])

    owned = rows // tc

    def compute(u):
        for flow in range(4, 8):
            c_copy(flow, u).wait_recv()
        local_c(u).wait()

        @pl.loop(0, nu // tile)
        def _(t):
            cols = pl.ds(pl.multiple_of(t * tile, tile), tile)
            total = jnp.zeros((rows, tile), jnp.float32)
            for q in range(dp):
                rhs = cbuf[u, q, :, :, cols].reshape(tr * ctok, tile)
                total += jnp.dot(at[q], rhs, preferred_element_type=jnp.float32)
            for j in range(tc):
                part = total[j * owned:(j + 1) * owned]
                obuf[u, j, :, cols] = encode(part)

                @pl.when(z == j)
                def _():
                    dbuf[u, j, :, cols] = part

        for j in range(1, tc):
            o_copy(j, u).start()
        store(z, 0, u).start()

    def finish(u):
        for j in range(1, tc):
            o_copy(j, u).wait_recv()
            block = lax.rem(z + tc - j, tc)

            @pl.loop(0, owned // 16)
            def _(i):
                part = pl.ds(pl.multiple_of(i * 16, 16), 16)
                dbuf[u, block, part] = decode(rbuf[u, block, part])

            store(block, j, u).start()

    for k in range(1, 4):
        a_dp(k).start()
    send_z(0, 0)
    for u in range(AHEAD):
        own(u)
    local_a.start()
    for u in range(chunks):
        local_c(u).start()
    for k in range(1, 4):
        a_dp(k).wait_recv()
        send_z(0, k)

    def forward(s, k):
        got_z(s - 1, k)
        send_z(s, k)

    def step_xy(u):
        got_xy(u)
        if u + AHEAD < chunks:
            own(u + AHEAD)

    def last_a(k):
        got_z(tc - 2, k)
        if k == 0:
            local_a.wait()
        at[rel[k]] = abuf[rel[k]].reshape(tc * atok, rows).T

    beat, turn = 4.4, 70.0 / chunks
    tasks = []
    for i in range(4 * (tc - 1)):
        s, k = i // 4 + 1, i % 4
        tasks.append((9 + beat * i, forward, (s, k)) if s < tc - 1 else (9 + beat * i, last_a, (k,)))
    ready = 9 + beat * 4 * (tc - 1)
    for u in range(chunks):
        seen = 9 + turn * (u + 0.67)
        tasks.append((seen, step_xy, (u,)))
        tasks.append((seen + turn, got_diag, (u,)))
        tasks.append((max(seen + turn, ready) + 0.1, compute, (u,)))
        tasks.append((max(ready + (u + 1) * 35.0 / chunks, seen + turn) + 6, finish, (u,)))
    for _, task, args in sorted(tasks, key=lambda entry: entry[0]):
        task(*args)

    for k in range(1, 4):
        a_dp(k).wait_send()
    for d in range(2):
        for s in range(tc - 1):
            @pl.when(a_z_sends(d, s))
            def _():
                for k in range(4):
                    a_z(d, s, k).wait_send()
    for u in range(chunks):
        for flow in range(8):
            c_copy(flow, u).wait_send()
    for u in range(chunks):
        store(z, 0, u).wait()
        for j in range(1, tc):
            o_copy(j, u).wait_send()
            store(lax.rem(z + tc - j, tc), j, u).wait()


def vmem_plan(activations, cotangent, dp, tr, tc):
    atok, features = activations.shape
    ctok, units = cotangent.shape
    rows = features // dp
    return dp * tc * atok * rows * 4 + dp * tr * ctok * units * 2 + rows * units * 8


def gathered(activations, cotangent, dp, tr, tc):
    atok, features = activations.shape
    ctok, units = cotangent.shape
    rows = features // dp
    owned = rows // tc
    chunks = CHUNKS
    nu = units // chunks
    tile = min(nu, 256)
    return pl.pallas_call(
        functools.partial(grad_kernel, (dp, tr, tc, chunks, tile)),
        out_shape=jax.ShapeDtypeStruct((owned, tc * units), jnp.float32),
        in_specs=[pl.BlockSpec(memory_space=pltpu.HBM)] * 2,
        out_specs=pl.BlockSpec(memory_space=pl.ANY),
        scratch_shapes=[
            pltpu.VMEM((dp, tc, atok, rows), jnp.bfloat16),
            pltpu.VMEM((chunks, dp, tr, ctok, nu), jnp.bfloat16),
            pltpu.VMEM((dp, rows, tc * atok), jnp.bfloat16),
            pltpu.VMEM((chunks, tc, owned, nu), jnp.bfloat16),
            pltpu.VMEM((chunks, tc, owned, nu), jnp.bfloat16),
            pltpu.VMEM((chunks, tc, owned, nu), jnp.float32),
            pltpu.SemaphoreType.DMA((1 + chunks,)),
            pltpu.SemaphoreType.DMA((4,)),
            pltpu.SemaphoreType.DMA((4,)),
            pltpu.SemaphoreType.DMA((2, tc - 1, 4)),
            pltpu.SemaphoreType.DMA((2, tc - 1, 4)),
            pltpu.SemaphoreType.DMA((8, chunks)),
            pltpu.SemaphoreType.DMA((8, chunks)),
            pltpu.SemaphoreType.DMA((tc, chunks)),
            pltpu.SemaphoreType.DMA((tc, chunks)),
            pltpu.SemaphoreType.DMA((tc, chunks)),
        ],
        compiler_params=pltpu.CompilerParams(
            collective_id=0, has_side_effects=True, vmem_limit_bytes=VMEM_BYTES
        ),
    )(activations, cotangent)


def native(activations, cotangent):
    act_rows = lax.all_gather(activations, "tc", axis=0, tiled=True)
    cot_rows = lax.all_gather(cotangent, "tr", axis=0, tiled=True)
    replicas = lax.axis_size("dp")
    columns = lax.axis_size("tc")
    feature_count = act_rows.shape[1]
    unit_count = cot_rows.shape[1]
    owned = feature_count // (replicas * columns)
    summed = lax.psum_scatter(
        lax.dot_general(
            act_rows, cot_rows, (((0,), (0,)), ((), ())), preferred_element_type=jnp.float32
        ),
        "dp",
        scatter_dimension=0,
        tiled=True,
    )
    summed = summed.reshape(columns, owned, unit_count)
    return lax.all_to_all(summed, "tc", split_axis=0, concat_axis=2, tiled=True)


def shards(activations, cotangent, master, moment, second):
    dp, tr, tc = (lax.axis_size(name) for name in ("dp", "tr", "tc"))
    small = vmem_plan(activations, cotangent, dp, tr, tc) < VMEM_BYTES * 7 // 8
    if dp == 4 and tr == 2 and tc > 2 and small:
        grad = gathered(activations, cotangent, dp, tr, tc)
        grad = grad.reshape(master.shape)
    else:
        grad = native(activations, cotangent)
    new_moment = first_decay * moment + (1.0 - first_decay) * grad
    new_second = second_decay * second + (1.0 - second_decay) * grad * grad
    update = new_moment / first_fix / (jnp.sqrt(new_second / second_fix) + epsilon)
    new_master = master - learn_rate * (update + weight_decay * master)
    return (new_master, new_moment, new_second)


def solution(mesh):
    return jax.shard_map(
        shards,
        mesh=mesh,
        in_specs=(
            P(("dp", "tc"), "tr"),
            P(("dp", "tr"), "tc"),
            P("tr", ("dp", "tc"), None),
            P("tr", ("dp", "tc"), None),
            P("tr", ("dp", "tc"), None),
        ),
        out_specs=(
            P("tr", ("dp", "tc"), None),
            P("tr", ("dp", "tc"), None),
            P("tr", ("dp", "tc"), None),
        ),
        check_vma=False,
    )
```

```python
import functools

import jax
import jax.numpy as jnp
from jax import lax
from jax.experimental import pallas as pl
from jax.experimental.pallas import tpu as pltpu
from jax.sharding import PartitionSpec as P

first_decay = 0.9
second_decay = 0.95
learn_rate = 0.0003
weight_decay = 0.1
epsilon = 1e-08
first_fix = 1.0 - 0.9**10
second_fix = 1.0 - 0.95**10

MESH = pl.DeviceIdType.MESH
VMEM_BYTES = 60 * 2**20
CHUNKS = 8
AHEAD = 2
EARLY = 2
LEVELS = 12.0
STEPS = 128.0 * LEVELS


def encode(v):
    y = jnp.abs(v) * 2.0**8
    tiny = y < 1.0
    y = jnp.where(tiny, y + 1.0, y)
    high = y >= 2.0**16
    power = jnp.where(high, 2.0**78, jnp.where(tiny, 2.0**-126, 2.0**-114))
    y = jnp.where(high, y * 2.0**-16, y)
    for s in (8, 4, 2, 1):
        big = y >= 2.0**s
        y = jnp.where(big, y * 2.0**-s, y)
        power = jnp.where(big, power * 2.0 ** (12 * s), power)
    step = jnp.minimum(jnp.floor((y - 1.0) * STEPS + 0.5), STEPS - 1.0)
    quotient = jnp.floor((step + 0.5) * (1.0 / LEVELS))
    rest = step - LEVELS * quotient
    for s in (8, 4, 2, 1):
        big = rest >= s
        rest = jnp.where(big, rest - s, rest)
        power = jnp.where(big, power * 2.0**s, power)
    code = power * (1.0 + quotient * (1.0 / 128.0))
    return jnp.where(v < 0.0, -code, code).astype(jnp.bfloat16)


def decode(code):
    code = code.astype(jnp.float32)
    x = jnp.abs(code)
    top, mid = x >= 2.0**66, x >= 2.0**-30
    x = x * jnp.where(top, 2.0**-66, jnp.where(mid, 2.0**30, 2.0**126))
    power = jnp.where(top, 2.0**15, jnp.where(mid, 2.0**7, 2.0**-1))
    for s in (4, 2, 1):
        big = x >= 2.0 ** (12 * s)
        x = jnp.where(big, x * 2.0 ** (-12 * s), x)
        power = jnp.where(big, power * 2.0**s, power)
    rest = jnp.zeros_like(x)
    for s in (8, 4, 2, 1):
        big = x >= 2.0**s
        x = jnp.where(big, x * 2.0**-s, x)
        rest = jnp.where(big, rest + s, rest)
    x = x + rest * (1.0 / STEPS)
    y = jnp.where(power < 1.0, x - 1.0, x * power) * 2.0**-8
    return jnp.where(code < 0.0, -y, y)


def grad_kernel(sizes, act, cot, out, abuf, cbuf, at, obuf, rbuf, dbuf, sums, ld_sem, adp_s, adp_r, az_s, az_r, c_s, c_r, o_s, o_r, st_sem):
    dp, tr, tc, chunks, tile = sizes
    r, c, z = lax.axis_index("dp"), lax.axis_index("tr"), lax.axis_index("tc")
    rx = r + 1 - 2 * lax.rem(r, 2)
    ry = lax.rem(r + 2, 4)
    rd = 3 - r
    rel = (r, rx, ry, rd)
    atok, rows = abuf.shape[2], abuf.shape[3]
    ctok, nu = cbuf.shape[3], cbuf.shape[4]
    units = chunks * nu
    half = ctok // 2

    barrier = pltpu.get_barrier_semaphore()
    peers = [{"dp": q} for q in (rx, ry, rd)] + [{"tr": 1 - c}]
    peers += [{"tc": lax.rem(z + j, tc)} for j in range(1, tc)]
    for peer in peers:
        pl.semaphore_signal(barrier, inc=1, device_id=peer, device_id_type=MESH)
    pl.semaphore_wait(barrier, len(peers))

    def remote(src, dst, s, d, peer):
        return pltpu.make_async_remote_copy(
            src_ref=src, dst_ref=dst, send_sem=s, recv_sem=d, device_id=peer, device_id_type=MESH
        )

    def act_cols(q):
        return act.at[:, pl.ds(pl.multiple_of(q * rows, 128), rows)]

    def a_dp(k):
        return remote(act_cols(rel[k]), abuf.at[r, z], adp_s.at[k], adp_r.at[k], {"dp": rel[k]})

    def a_z(d, s, k):
        block = z - s if d == 0 else z + s
        to = z + 1 if d == 0 else z - 1
        slot = abuf.at[rel[k], block]
        src = act_cols(r) if s == 0 and k == 0 else slot
        return remote(src, slot, az_s.at[d, s, k], az_r.at[d, s, k], {"tc": to})

    def a_z_sends(d, s):
        return (z >= s) & (z < tc - 1) if d == 0 else (z < tc - s) & (z > 0)

    def a_z_gets(d, s):
        return z >= s + 1 if d == 0 else z < tc - 1 - s

    def send_z(s, k):
        for d in range(2):
            @pl.when(a_z_sends(d, s))
            def _():
                a_z(d, s, k).start()

    def got_z(s, k):
        for d in range(2):
            @pl.when(a_z_gets(d, s))
            def _():
                a_z(d, s, k).wait_recv()

    def cot_cols(u):
        return cot.at[:, pl.ds(u * nu, nu)]

    def c_copy(flow, u):
        if flow == 0:
            return remote(cot_cols(u), cbuf.at[u, r, c], c_s.at[0, u], c_r.at[0, u], {"dp": rx})
        if flow == 1:
            return remote(cot_cols(u), cbuf.at[u, r, c], c_s.at[1, u], c_r.at[1, u], {"dp": ry})
        if flow == 2:
            part = cbuf.at[u, ry, c, pl.ds(0, half)]
            return remote(part, part, c_s.at[2, u], c_r.at[2, u], {"dp": rx})
        if flow == 3:
            part = cbuf.at[u, rx, c, pl.ds(half, half)]
            return remote(part, part, c_s.at[3, u], c_r.at[3, u], {"dp": ry})
        k = flow - 4
        slot = cbuf.at[u, rel[k], c]
        src = cot_cols(u) if k == 0 else slot
        return remote(src, slot, c_s.at[flow, u], c_r.at[flow, u], {"tr": 1 - c})

    def own(u):
        for flow in (0, 1, 4):
            c_copy(flow, u).start()

    def got_xy(u):
        c_copy(0, u).wait_recv()
        c_copy(3, u).start()
        c_copy(5, u).start()
        c_copy(1, u).wait_recv()
        c_copy(2, u).start()
        c_copy(6, u).start()

    def got_diag(u):
        c_copy(2, u).wait_recv()
        c_copy(3, u).wait_recv()
        c_copy(7, u).start()

    def local_c(u):
        return pltpu.make_async_copy(cot_cols(u), cbuf.at[u, r, c], ld_sem.at[1 + u])

    local_a = pltpu.make_async_copy(act_cols(r), abuf.at[r, z], ld_sem.at[0])

    def o_copy(j, u):
        to = lax.rem(z + j, tc)
        return remote(obuf.at[u, to], rbuf.at[u, z], o_s.at[j, u], o_r.at[j, u], {"tc": to})

    def store(block, j, u):
        dst = out.at[:, pl.ds(pl.multiple_of(block * units + u * nu, 128), nu)]
        return pltpu.make_async_copy(dbuf.at[u, block], dst, st_sem.at[j, u])

    owned = rows // tc

    def product(q, u, cols):
        rhs = cbuf[u, q, :, :, cols].reshape(tr * ctok, tile)
        return jnp.dot(at[q], rhs, preferred_element_type=jnp.float32)

    def partial(k, u):
        c_copy(4 + k, u).wait_recv()
        if k == 0:
            local_c(u).wait()

        @pl.loop(0, nu // tile)
        def _(t):
            cols = pl.ds(pl.multiple_of(t * tile, tile), tile)
            term = product(rel[k], u, cols)
            sums[u, :, cols] = term if k == 0 else sums[u, :, cols] + term

    def compute(u):
        for flow in range(7 if u < EARLY else 4, 8):
            c_copy(flow, u).wait_recv()
        if u >= EARLY:
            local_c(u).wait()

        @pl.loop(0, nu // tile)
        def _(t):
            cols = pl.ds(pl.multiple_of(t * tile, tile), tile)
            if u < EARLY:
                total = sums[u, :, cols] + product(rel[3], u, cols)
            else:
                total = jnp.zeros((rows, tile), jnp.float32)
                for q in range(dp):
                    total += product(q, u, cols)
            for j in range(tc):
                part = total[j * owned:(j + 1) * owned]
                obuf[u, j, :, cols] = encode(part)

                @pl.when(z == j)
                def _():
                    dbuf[u, j, :, cols] = part

        for j in (2, 1, *range(3, tc)):
            o_copy(j, u).start()
        store(z, 0, u).start()

    def finish(u):
        for j in range(1, tc):
            o_copy(j, u).wait_recv()
            block = lax.rem(z + tc - j, tc)

            @pl.loop(0, owned // 16)
            def _(i):
                part = pl.ds(pl.multiple_of(i * 16, 16), 16)
                dbuf[u, block, part] = decode(rbuf[u, block, part])

            store(block, j, u).start()

    for k in range(1, 4):
        a_dp(k).start()
    send_z(0, 0)
    for u in range(AHEAD):
        own(u)
    local_a.start()
    for u in range(chunks):
        local_c(u).start()
    for k in range(1, 4):
        a_dp(k).wait_recv()
        send_z(0, k)

    def forward(s, k):
        got_z(s - 1, k)
        send_z(s, k)

    def step_xy(u):
        got_xy(u)
        if u + AHEAD < chunks:
            own(u + AHEAD)

    def last_a(k):
        got_z(tc - 2, k)
        if k == 0:
            local_a.wait()
        at[rel[k]] = abuf[rel[k]].reshape(tc * atok, rows).T
        if k < 3:
            for u in range(EARLY):
                partial(k, u)

    beat, turn = 4.4, 70.0 / chunks
    tasks = []
    for i in range(4 * (tc - 1)):
        s, k = i // 4 + 1, i % 4
        tasks.append((9 + beat * i, forward, (s, k)) if s < tc - 1 else (9 + beat * i, last_a, (k,)))
    ready = 9 + beat * 4 * (tc - 1)
    for u in range(chunks):
        seen = 9 + turn * (u + 0.67)
        tasks.append((seen, step_xy, (u,)))
        tasks.append((seen + turn, got_diag, (u,)))
        tasks.append((max(seen + turn, ready) + 0.1, compute, (u,)))
        tasks.append((max(ready + (u + 1) * 35.0 / chunks, seen + turn) + 6, finish, (u,)))
    for _, task, args in sorted(tasks, key=lambda entry: entry[0]):
        task(*args)

    for k in range(1, 4):
        a_dp(k).wait_send()
    for d in range(2):
        for s in range(tc - 1):
            @pl.when(a_z_sends(d, s))
            def _():
                for k in range(4):
                    a_z(d, s, k).wait_send()
    for u in range(chunks):
        for flow in range(8):
            c_copy(flow, u).wait_send()
    for u in range(chunks):
        store(z, 0, u).wait()
        for j in range(1, tc):
            o_copy(j, u).wait_send()
            store(lax.rem(z + tc - j, tc), j, u).wait()


def vmem_plan(activations, cotangent, dp, tr, tc):
    atok, features = activations.shape
    ctok, units = cotangent.shape
    rows = features // dp
    return dp * tc * atok * rows * 4 + dp * tr * ctok * units * 2 + rows * units * 8


def gathered(activations, cotangent, dp, tr, tc):
    atok, features = activations.shape
    ctok, units = cotangent.shape
    rows = features // dp
    owned = rows // tc
    chunks = CHUNKS
    nu = units // chunks
    tile = min(nu, 256)
    return pl.pallas_call(
        functools.partial(grad_kernel, (dp, tr, tc, chunks, tile)),
        out_shape=jax.ShapeDtypeStruct((owned, tc * units), jnp.float32),
        in_specs=[pl.BlockSpec(memory_space=pltpu.HBM)] * 2,
        out_specs=pl.BlockSpec(memory_space=pl.ANY),
        scratch_shapes=[
            pltpu.VMEM((dp, tc, atok, rows), jnp.bfloat16),
            pltpu.VMEM((chunks, dp, tr, ctok, nu), jnp.bfloat16),
            pltpu.VMEM((dp, rows, tc * atok), jnp.bfloat16),
            pltpu.VMEM((chunks, tc, owned, nu), jnp.bfloat16),
            pltpu.VMEM((chunks, tc, owned, nu), jnp.bfloat16),
            pltpu.VMEM((chunks, tc, owned, nu), jnp.float32),
            pltpu.VMEM((EARLY, rows, nu), jnp.float32),
            pltpu.SemaphoreType.DMA((1 + chunks,)),
            pltpu.SemaphoreType.DMA((4,)),
            pltpu.SemaphoreType.DMA((4,)),
            pltpu.SemaphoreType.DMA((2, tc - 1, 4)),
            pltpu.SemaphoreType.DMA((2, tc - 1, 4)),
            pltpu.SemaphoreType.DMA((8, chunks)),
            pltpu.SemaphoreType.DMA((8, chunks)),
            pltpu.SemaphoreType.DMA((tc, chunks)),
            pltpu.SemaphoreType.DMA((tc, chunks)),
            pltpu.SemaphoreType.DMA((tc, chunks)),
        ],
        compiler_params=pltpu.CompilerParams(
            collective_id=0, has_side_effects=True, vmem_limit_bytes=VMEM_BYTES
        ),
    )(activations, cotangent)


def native(activations, cotangent):
    act_rows = lax.all_gather(activations, "tc", axis=0, tiled=True)
    cot_rows = lax.all_gather(cotangent, "tr", axis=0, tiled=True)
    replicas = lax.axis_size("dp")
    columns = lax.axis_size("tc")
    feature_count = act_rows.shape[1]
    unit_count = cot_rows.shape[1]
    owned = feature_count // (replicas * columns)
    summed = lax.psum_scatter(
        lax.dot_general(
            act_rows, cot_rows, (((0,), (0,)), ((), ())), preferred_element_type=jnp.float32
        ),
        "dp",
        scatter_dimension=0,
        tiled=True,
    )
    summed = summed.reshape(columns, owned, unit_count)
    return lax.all_to_all(summed, "tc", split_axis=0, concat_axis=2, tiled=True)


def shards(activations, cotangent, master, moment, second):
    dp, tr, tc = (lax.axis_size(name) for name in ("dp", "tr", "tc"))
    small = vmem_plan(activations, cotangent, dp, tr, tc) < VMEM_BYTES * 3 // 4
    if dp == 4 and tr == 2 and tc > 2 and small:
        grad = gathered(activations, cotangent, dp, tr, tc)
        grad = grad.reshape(master.shape)
    else:
        grad = native(activations, cotangent)
    new_moment = first_decay * moment + (1.0 - first_decay) * grad
    new_second = second_decay * second + (1.0 - second_decay) * grad * grad
    update = new_moment / first_fix / (jnp.sqrt(new_second / second_fix) + epsilon)
    new_master = master - learn_rate * (update + weight_decay * master)
    return (new_master, new_moment, new_second)


def solution(mesh):
    return jax.shard_map(
        shards,
        mesh=mesh,
        in_specs=(
            P(("dp", "tc"), "tr"),
            P(("dp", "tr"), "tc"),
            P("tr", ("dp", "tc"), None),
            P("tr", ("dp", "tc"), None),
            P("tr", ("dp", "tc"), None),
        ),
        out_specs=(
            P("tr", ("dp", "tc"), None),
            P("tr", ("dp", "tc"), None),
            P("tr", ("dp", "tc"), None),
        ),
        check_vma=False,
    )
```
